32 devices in a mesh: dp: 4 (over z), seq: 4 (over y, x), head: 2 (over core).
Axes of the slice: x: 2, y: 2, z: 4, core: 2. Of those that a mesh axis runs over, the one named last changes fastest.
Arguments:
- hidden: bfloat16 [4, 1024, 768], P('dp', 'seq'), may hold values from -6 to 6
- cotangent: bfloat16 [4, 1024, 768], P('dp', 'seq'), may hold values from -6 to 6
- norm_gain: float32 [768], replicated, may hold values from 0.5 to 1.5
- w_zx: float32 [768, 2, 1536], P(('dp', 'seq'), None, 'head'), may hold values from -0.21875 to 0.21875
- w_bc: float32 [768, 256], P(('dp', 'seq')), may hold values from -0.21875 to 0.21875
- dt_table: float32 [771, 24], P(None, 'head'), may hold values from -9 to 1.5, as said below
- x_conv: float32 [6, 1536], P(None, 'head'), may hold values from -3 to 3
- bc_conv: float32 [5, 256], replicated, may hold values from -3 to 3
- w_out: float32 [1536, 768], P('head', ('dp', 'seq')), may hold values from -0.15625 to 0.15625
- mom_norm: float32 [2, 768], replicated, may hold values from -8 to 20, as said below
- mom_zx: float32 [2, 768, 2, 1536], P(None, ('dp', 'seq'), None, 'head'), may hold values from -8 to 20, as said below
- mom_bc: float32 [2, 768, 256], P(None, ('dp', 'seq')), may hold values from -8 to 20, as said below
- mom_table: float32 [2, 771, 24], P(None, None, 'head'), may hold values from -8 to 20, as said below
- mom_xconv: float32 [2, 6, 1536], P(None, None, 'head'), may hold values from -8 to 20, as said below
- mom_bcconv: float32 [2, 5, 256], replicated, may hold values from -8 to 20, as said below
- mom_out: float32 [2, 1536, 768], P(None, 'head', ('dp', 'seq')), may hold values from -8 to 20, as said below
Outputs:
- output: bfloat16 [4, 1024, 768], P('dp', 'seq')
- d_hidden: float32 [4, 1024, 768], P('dp', 'seq')
- grad_norm: float32 [768], replicated
- grad_zx: float32 [768, 2, 1536], P(('dp', 'seq'), None, 'head')
- grad_bc: float32 [768, 256], P(('dp', 'seq'))
- grad_table: float32 [771, 24], P(None, 'head')
- grad_xconv: float32 [6, 1536], P(None, 'head')
- grad_bcconv: float32 [5, 256], replicated
- grad_out: float32 [1536, 768], P('head', ('dp', 'seq'))
- new_norm: float32 [768], replicated
- new_zx: float32 [768, 2, 1536], P(('dp', 'seq'), None, 'head')
- new_bc: float32 [768, 256], P(('dp', 'seq'))
- new_table: float32 [771, 24], P(None, 'head')
- new_xconv: float32 [6, 1536], P(None, 'head')
- new_bcconv: float32 [5, 256], replicated
- new_out: float32 [1536, 768], P('head', ('dp', 'seq'))
- new_mom_norm: float32 [2, 768], replicated
- new_mom_zx: float32 [2, 768, 2, 1536], P(None, ('dp', 'seq'), None, 'head')
- new_mom_bc: float32 [2, 768, 256], P(None, ('dp', 'seq'))
- new_mom_table: float32 [2, 771, 24], P(None, None, 'head')
- new_mom_xconv: float32 [2, 6, 1536], P(None, None, 'head')
- new_mom_bcconv: float32 [2, 5, 256], replicated
- new_mom_out: float32 [2, 1536, 768], P(None, 'head', ('dp', 'seq'))
The draws below stay inside these ranges and needn't reach their ends.
Inputs may be any that keep to these rules, and one draw needn't show every extreme that they name: `dt_table`: rows below 768 are small projection weights; the last three rows hold step biases, log rates and skip coefficients. `mom_norm`: row 0 real-valued, row 1 positive. `mom_zx`: row 0 real-valued, row 1 positive. `mom_bc`: row 0 real-valued, row 1 positive. `mom_table`: row 0 real-valued, row 1 positive. `mom_xconv`: row 0 real-valued, row 1 positive. `mom_bcconv`: row 0 real-valued, row 1 positive. `mom_out`: row 0 real-valued, row 1 positive.
All inputs are finite; a program needn't handle non-finite values.
Results may differ from the reference program's by a relative error of at most 0.011.
Values may be sent and summed in bfloat16 or wider, within the bound.
A program may use at most 128 MiB of HBM per device.

```python
import math
import jax
import jax.numpy as jnp
from jax import lax

D = 768
E = 1536
H = 24
N = 128
CONV = 4
BLOCK = 256
SEQS = 4
LEN = 1024


def moment_pair(key, shape):
    key_one = jax.random.fold_in(key, 11)
    key_two = jax.random.fold_in(key, 12)
    moment_one = 2.0 * jnp.clip(jax.random.normal(key_one, shape, jnp.float32), -4.0, 4.0)
    root_two = jnp.exp(jax.random.uniform(key_two, shape, jnp.float32, 0.0, math.log(20.0)))
    return jnp.stack([moment_one, root_two])


def draw_dt_table(key, part):
    key_proj = jax.random.fold_in(key, 21)
    key_bias = jax.random.fold_in(key, 22)
    key_rate = jax.random.fold_in(key, 23)
    key_skip = jax.random.fold_in(key, 24)
    projection = jnp.clip(jax.random.normal(key_proj, (D, H), jnp.float32), -4.0, 4.0) / math.sqrt(D)
    step_bias = jax.random.uniform(key_bias, (1, H), jnp.float32, -9.0, -3.0)
    log_rate = jax.random.uniform(key_rate, (1, H), jnp.float32, -1.0, 1.0)
    skip_coef = jax.random.uniform(key_skip, (1, H), jnp.float32, 0.5, 1.5)
    return jnp.concatenate([projection, step_bias, log_rate, skip_coef], axis=0)


def draw_mom_norm(key, part):
    return moment_pair(key, (D,))


def draw_mom_zx(key, part):
    return moment_pair(key, (D, 2, E))


def draw_mom_bc(key, part):
    return moment_pair(key, (D, 2 * N))


def draw_mom_table(key, part):
    return moment_pair(key, (D + 3, H))


def draw_mom_xconv(key, part):
    return moment_pair(key, (CONV + 2, E))


def draw_mom_bcconv(key, part):
    return moment_pair(key, (CONV + 1, 2 * N))


def draw_mom_out(key, part):
    return moment_pair(key, (E, D))


def levels(rng, dims, shards, low, largest):
    def one(position, parts):
        steps = jax.random.uniform(jax.random.fold_in(jax.random.fold_in(rng, 6), position), (parts,), jnp.float32, low / len(shards), largest / len(shards))
        return jnp.repeat(jnp.exp(steps), dims[position] // parts).reshape((-1,) + (1,) * (len(dims) - position - 1))

    loudness = one(*shards[0])
    for cut in shards[1:]:
        loudness = loudness * one(*cut)
    return loudness


def centred(key, shape, scale, limit, cuts=(), kind=jnp.bfloat16):
    array = jax.random.normal(key, shape, jnp.float32) * scale
    if len(cuts) > 0:
        array = levels(key, shape, cuts, -0.22, 0.18) * array
    return jnp.clip(array, min=-limit, max=limit).astype(kind)


def setup_inputs(seed: int = 0) -> dict:
    arg_keys = jax.random.split(jax.random.key(seed), 17)
    return {
        "hidden": centred(arg_keys[0], (SEQS, LEN, D), 1.0, 6.0, ((0, 4), (1, 4))),
        "cotangent": centred(arg_keys[1], (SEQS, LEN, D), 1.0, 6.0, ((0, 4), (1, 4))),
        "norm_gain": jnp.clip(1.0 + 0.1 * jax.random.normal(arg_keys[2], (D,), jnp.float32), 0.5, 1.5),
        "w_zx": centred(arg_keys[3], (D, 2, E), D ** -0.5, 0.21875, ((0, 16), (2, 2)), jnp.float32),
        "w_bc": centred(arg_keys[4], (D, 2 * N), D ** -0.5, 0.21875, ((0, 16),), jnp.float32),
        "dt_table": draw_dt_table(jax.random.fold_in(arg_keys[16], 71), 0),
        "x_conv": centred(arg_keys[6], (CONV + 2, E), 0.5, 3.0, ((1, 2),), jnp.float32),
        "bc_conv": centred(arg_keys[7], (CONV + 1, 2 * N), 0.5, 3.0, (), jnp.float32),
        "w_out": centred(arg_keys[8], (E, D), E ** -0.5, 0.15625, ((0, 2), (1, 16)), jnp.float32),
        "mom_norm": draw_mom_norm(jax.random.fold_in(arg_keys[16], 71), 0),
        "mom_zx": draw_mom_zx(jax.random.fold_in(arg_keys[16], 71), 0),
        "mom_bc": draw_mom_bc(jax.random.fold_in(arg_keys[16], 71), 0),
        "mom_table": draw_mom_table(jax.random.fold_in(arg_keys[16], 71), 0),
        "mom_xconv": draw_mom_xconv(jax.random.fold_in(arg_keys[16], 71), 0),
        "mom_bcconv": draw_mom_bcconv(jax.random.fold_in(arg_keys[16], 71), 0),
        "mom_out": draw_mom_out(jax.random.fold_in(arg_keys[16], 71), 0),
    }


norm_eps = 1e-05
learn_rate = 0.01
beta_one = 0.9
beta_two = 0.95
adam_eps = 1e-08
decay_weight = 0.1
adam_step = 10.0
far_below = -1e+30
highest = lax.Precision.HIGHEST

def conv_silu(signal, halo_rows, taps, shift_bias):
    padded = jnp.concatenate([halo_rows, signal], axis=0)
    length = signal.shape[0]
    total = jnp.broadcast_to(shift_bias[None, :], signal.shape)
    for offset in range(taps.shape[0]):
        total = total + taps[offset][None, :] * padded[offset:offset + length]
    return jax.nn.silu(total)

def block_step(state, block_data):
    x_block, b_block, c_block, dt_block, log_block = block_data
    cum_log = jnp.cumsum(log_block, axis=0)
    length = x_block.shape[0]
    row_ids = lax.broadcasted_iota(jnp.int32, (length, length), 0)
    col_ids = lax.broadcasted_iota(jnp.int32, (length, length), 1)
    causal = (row_ids >= col_ids)[:, :, None]
    spread = cum_log[:, None, :] - cum_log[None, :, :]
    decay_mat = jnp.exp(jnp.where(causal, spread, far_below))
    inner = jnp.dot(c_block, b_block.T, precision=highest)
    mixing = inner[:, :, None] * decay_mat * dt_block[None, :, :]
    y_block = jnp.einsum('tsh,shp->thp', mixing, x_block, precision=highest)
    carried = jnp.einsum('tn,hpn->thp', c_block, state, precision=highest)
    y_block = y_block + jnp.exp(cum_log)[:, :, None] * carried
    tail_weight = jnp.exp(cum_log[-1][None, :] - cum_log) * dt_block
    fresh = jnp.einsum('sh,shp,sn->hpn', tail_weight, x_block, b_block, precision=highest)
    new_state = jnp.exp(cum_log[-1])[:, None, None] * state + fresh
    return (new_state, y_block)

def ssd_run(inputs_x, b_mat, c_mat, dt_val, log_decay, start_state):
    tokens, num_heads, head_dim = inputs_x.shape
    blocks = tokens // BLOCK
    pieces = (inputs_x.reshape(blocks, BLOCK, num_heads, head_dim), b_mat.reshape(blocks, BLOCK, b_mat.shape[1]), c_mat.reshape(blocks, BLOCK, c_mat.shape[1]), dt_val.reshape(blocks, BLOCK, num_heads), log_decay.reshape(blocks, BLOCK, num_heads))
    final_state, outputs = lax.scan(block_step, start_state, pieces)
    return (outputs.reshape(tokens, num_heads, head_dim), final_state)

def mixer(proj_x, proj_bc, gate_z, dt_raw, x_conv, bc_conv, dt_small):
    tokens, inner_width = proj_x.shape
    num_heads = dt_small.shape[1]
    head_dim = inner_width // num_heads
    x_halo = jnp.zeros((CONV - 1, inner_width), jnp.float32)
    bc_halo = jnp.zeros((CONV - 1, proj_bc.shape[1]), jnp.float32)
    xs = conv_silu(proj_x, x_halo, x_conv[:CONV], x_conv[CONV]).reshape(tokens, num_heads, head_dim)
    bcs = conv_silu(proj_bc, bc_halo, bc_conv[:CONV], bc_conv[CONV])
    dt_val = jax.nn.softplus(dt_raw + dt_small[0][None, :])
    log_decay = -jnp.exp(dt_small[1])[None, :] * dt_val
    start = jnp.zeros((num_heads, head_dim, N), jnp.float32)
    y_ssd, _ = ssd_run(xs, bcs[:, :N], bcs[:, N:], dt_val, log_decay, start)
    y_all = y_ssd + dt_small[2][None, :, None] * xs
    return y_all.reshape(tokens, inner_width) * jax.nn.silu(gate_z)

def one_sequence(hidden_seq, cot_seq, weights):
    norm_gain, w_zx, w_bc, dt_table, x_conv, bc_conv, w_out = weights
    resid = hidden_seq.astype(jnp.float32)
    inv_rms = lax.rsqrt(lax.optimization_barrier(jnp.mean(resid * resid, axis=-1, keepdims=True)) + norm_eps)
    normed = (resid * inv_rms * norm_gain[None, :]).astype(jnp.bfloat16)
    zx_mat = w_zx.reshape(D, 2 * E).astype(jnp.bfloat16)
    bc_mat = w_bc.astype(jnp.bfloat16)
    dt_mat = dt_table[:D].astype(jnp.bfloat16)
    out_mat = w_out.astype(jnp.bfloat16)
    proj_zx = jnp.dot(normed, zx_mat, preferred_element_type=jnp.float32)
    gate_z = proj_zx[:, :E]
    proj_x = proj_zx[:, E:]
    proj_bc = jnp.dot(normed, bc_mat, preferred_element_type=jnp.float32)
    dt_raw = jnp.dot(normed, dt_mat, preferred_element_type=jnp.float32)
    dt_small = dt_table[D:]
    gated, pull = jax.vjp(mixer, proj_x, proj_bc, gate_z, dt_raw, x_conv, bc_conv, dt_small)
    squares = lax.optimization_barrier(jnp.sum(gated * gated, axis=-1, keepdims=True))
    inv_g = lax.rsqrt(squares / E + norm_eps)
    gain_g = 1.0 + x_conv[CONV + 1][None, :]
    mixed = (gated * inv_g * gain_g).astype(jnp.bfloat16)
    branch = jnp.dot(mixed, out_mat, preferred_element_type=jnp.float32)
    output = (resid + branch).astype(jnp.bfloat16)
    d_mixed = jnp.dot(cot_seq, out_mat.T, preferred_element_type=jnp.float32)
    grad_out = jnp.dot(mixed.T, cot_seq, preferred_element_type=jnp.float32)
    scaled = d_mixed * gain_g
    gain_grad = lax.optimization_barrier(jnp.sum(d_mixed * gated * inv_g, axis=0))
    d_gated = inv_g * scaled - gated * inv_g ** 3 / E * lax.optimization_barrier(jnp.sum(scaled * gated, axis=-1, keepdims=True))
    d_px, d_pbc, d_gz, d_dr, g_xconv, g_bcconv, g_small = pull(d_gated)
    d_zx = jnp.concatenate([d_gz, d_px], axis=1).astype(jnp.bfloat16)
    d_bc = d_pbc.astype(jnp.bfloat16)
    d_dt = d_dr.astype(jnp.bfloat16)
    grad_zx = jnp.dot(normed.T, d_zx, preferred_element_type=jnp.float32).reshape(D, 2, E)
    grad_bc = jnp.dot(normed.T, d_bc, preferred_element_type=jnp.float32)
    grad_dt = jnp.dot(normed.T, d_dt, preferred_element_type=jnp.float32)
    d_normed = jnp.dot(d_zx, zx_mat.T, preferred_element_type=jnp.float32) + jnp.dot(d_bc, bc_mat.T, preferred_element_type=jnp.float32) + jnp.dot(d_dt, dt_mat.T, preferred_element_type=jnp.float32)
    grad_norm = lax.optimization_barrier(jnp.sum(d_normed * resid * inv_rms, axis=0))
    scaled_n = d_normed * norm_gain[None, :]
    d_hidden = cot_seq.astype(jnp.float32) + inv_rms * scaled_n - resid * inv_rms ** 3 / D * lax.optimization_barrier(jnp.sum(scaled_n * resid, axis=-1, keepdims=True))
    grad_xconv = jnp.concatenate([g_xconv[:CONV + 1], g_xconv[CONV + 1:] + gain_grad[None, :]], axis=0)
    grad_table = jnp.concatenate([grad_dt, g_small], axis=0)
    grads = (grad_norm, grad_zx, grad_bc, grad_table, grad_xconv, g_bcconv, grad_out)
    return (output, d_hidden, grads)

def adamw(weight, moments, grad):
    moment_one = beta_one * moments[0] + (1.0 - beta_one) * grad
    root_two = jnp.sqrt(beta_two * moments[1] * moments[1] + (1.0 - beta_two) * grad * grad)
    first_hat = moment_one / (1.0 - beta_one ** adam_step)
    root_hat = root_two / (1.0 - beta_two ** adam_step) ** 0.5
    updated = weight - learn_rate * (first_hat / (root_hat + adam_eps) + decay_weight * weight)
    return (updated, jnp.stack([moment_one, root_two]))

def reference(hidden, cotangent, norm_gain, w_zx, w_bc, dt_table, x_conv, bc_conv, w_out, mom_norm, mom_zx, mom_bc, mom_table, mom_xconv, mom_bcconv, mom_out):
    weights = (norm_gain, w_zx, w_bc, dt_table, x_conv, bc_conv, w_out)
    zero_grads = tuple((jnp.zeros(item.shape, jnp.float32) for item in weights))

    def seq_step(carry, pair):
        out_seq, dh_seq, grads = one_sequence(pair[0], pair[1], weights)
        return (tuple((acc + new_g for acc, new_g in zip(carry, grads))), (out_seq, dh_seq))
    grads, stacked = lax.scan(seq_step, zero_grads, (hidden, cotangent))
    output, d_hidden = stacked
    g_norm, g_zx, g_bc, g_table, g_xconv, g_bcconv, g_out = grads
    new_norm, new_mom_norm = adamw(norm_gain, mom_norm, g_norm)
    new_zx, new_mom_zx = adamw(w_zx, mom_zx, g_zx)
    new_bc, new_mom_bc = adamw(w_bc, mom_bc, g_bc)
    new_table, new_mom_table = adamw(dt_table, mom_table, g_table)
    new_xconv, new_mom_xconv = adamw(x_conv, mom_xconv, g_xconv)
    new_bcconv, new_mom_bcconv = adamw(bc_conv, mom_bcconv, g_bcconv)
    new_out, new_mom_out = adamw(w_out, mom_out, g_out)
    return (output, d_hidden, g_norm, g_zx, g_bc, g_table, g_xconv, g_bcconv, g_out, new_norm, new_zx, new_bc, new_table, new_xconv, new_bcconv, new_out, new_mom_norm, new_mom_zx, new_mom_bc, new_mom_table, new_mom_xconv, new_mom_bcconv, new_mom_out)
```

```python
import jax
import jax.numpy as jnp
from jax import lax
from jax.sharding import PartitionSpec as P

D = 768
E = 1536
N = 128
CONV = 4
BLOCK = 256


norm_eps = 1e-05
learn_rate = 0.01
beta_one = 0.9
beta_two = 0.95
adam_eps = 1e-08
decay_weight = 0.1
adam_step = 10.0
far_below = -1e30
highest = lax.Precision.HIGHEST


def from_behind(block, axis, distance):
    devices = range(lax.axis_size(axis))
    route = [(i - distance, i) for i in devices if i - distance in devices]
    return lax.ppermute(block, axis, route)


def turn(block, axis, distance):
    count = lax.axis_size(axis)
    return lax.ppermute(block, axis, [(i, (i + distance) % count) for i in range(count)])


def gather_axis(block, axis):
    count = lax.axis_size(axis)
    place = lax.axis_index(axis)
    whole = jnp.zeros((count,) + block.shape, block.dtype)
    for distance in range(count):
        part = turn(block, axis, distance) if distance else block
        source = lax.rem(place - distance + count, count)
        whole = lax.dynamic_update_index_in_dim(whole, part, source, 0)
    return whole


def scatter_axis(blocks, axis):
    count = lax.axis_size(axis)
    place = lax.axis_index(axis)
    total = None
    for distance in range(count):
        target = lax.rem(place + distance, count)
        part = lax.dynamic_index_in_dim(blocks, target, 0, False)
        part = turn(part.astype(jnp.bfloat16), axis, distance) if distance else part
        part = part.astype(jnp.float32)
        total = part if total is None else total + part
    return total


def sum_axis(block, axis):
    total = block
    for distance in range(1, lax.axis_size(axis)):
        total = total + turn(block, axis, distance)
    return total


def after(block, other):
    return lax.optimization_barrier((block, other))[0]


def spread_rows(stage_one):
    by_seq = gather_axis(stage_one, "seq")
    return jnp.swapaxes(by_seq, 0, 1).reshape(-1, stage_one.shape[-1])


def scatter_rows(grads):
    dp, seq = lax.axis_size("dp"), lax.axis_size("seq")
    blocks = grads.reshape(dp, seq, grads.shape[0] // (dp * seq), grads.shape[1])
    by_seq = scatter_axis(jnp.swapaxes(blocks, 0, 1), "seq")
    return scatter_axis(by_seq, "dp")


def with_partner(block):
    return block + turn(block, "head", 1)


def entering(decays, state, axis, reverse):
    sign = -1 if reverse else 1
    distances = range(1, lax.axis_size(axis))
    sent = state.astype(jnp.bfloat16)
    states = [from_behind(sent, axis, sign * d).astype(jnp.float32) for d in distances]
    place = lax.axis_index(axis)
    total = jnp.zeros_like(state)
    for d in reversed(distances):
        source = jnp.clip(place - sign * d, 0, lax.axis_size(axis) - 1)
        passed = lax.dynamic_index_in_dim(decays, source, 0, False)
        total = passed[..., None, None] * total + states[d - 1]
    return total


def conv_silu(signal, halo_rows, taps, shift_bias):
    padded = jnp.concatenate([halo_rows, signal], axis=0)
    length = signal.shape[0]
    total = jnp.broadcast_to(shift_bias[None, :], signal.shape)
    for offset in range(taps.shape[0]):
        total = total + taps[offset][None, :] * padded[offset : offset + length]
    return jax.nn.silu(total)


def block_step(state, block_data):
    x_block, b_block, c_block, dt_block, log_block = block_data
    cum_log = jnp.cumsum(log_block, axis=0)
    length = x_block.shape[0]
    row_ids = lax.broadcasted_iota(jnp.int32, (length, length), 0)
    col_ids = lax.broadcasted_iota(jnp.int32, (length, length), 1)
    causal = (row_ids >= col_ids)[:, :, None]
    spread = cum_log[:, None, :] - cum_log[None, :, :]
    decay_mat = jnp.exp(jnp.where(causal, spread, far_below))
    inner = jnp.dot(c_block, b_block.T, precision=highest)
    mixing = inner[:, :, None] * decay_mat * dt_block[None, :, :]
    y_block = jnp.einsum("tsh,shp->thp", mixing, x_block, precision=highest)
    carried = jnp.einsum("tn,hpn->thp", c_block, state, precision=highest)
    y_block = y_block + jnp.exp(cum_log)[:, :, None] * carried
    tail_weight = jnp.exp(cum_log[-1][None, :] - cum_log) * dt_block
    fresh = jnp.einsum("sh,shp,sn->hpn", tail_weight, x_block, b_block, precision=highest)
    new_state = jnp.exp(cum_log[-1])[:, None, None] * state + fresh
    return (new_state, y_block)


def ssd_run(inputs_x, b_mat, c_mat, dt_val, log_decay, start_state):
    tokens, num_heads, head_dim = inputs_x.shape
    blocks = tokens // BLOCK
    pieces = (
        inputs_x.reshape(blocks, BLOCK, num_heads, head_dim),
        b_mat.reshape(blocks, BLOCK, b_mat.shape[1]),
        c_mat.reshape(blocks, BLOCK, c_mat.shape[1]),
        dt_val.reshape(blocks, BLOCK, num_heads),
        log_decay.reshape(blocks, BLOCK, num_heads),
    )
    final_state, outputs = lax.scan(block_step, start_state, pieces)
    return (outputs.reshape(tokens, num_heads, head_dim), final_state)


def prepare(proj_x, proj_bc, halo_rows, x_conv, bc_conv, dt_small, dt_raw):
    tokens, inner_width = proj_x.shape
    num_heads = dt_small.shape[1]
    xs = conv_silu(proj_x, halo_rows[:, :inner_width], x_conv[:CONV], x_conv[CONV])
    xs = xs.reshape(tokens, num_heads, inner_width // num_heads)
    bcs = conv_silu(proj_bc, halo_rows[:, inner_width:], bc_conv[:CONV], bc_conv[CONV])
    dt_val = jax.nn.softplus(dt_raw + dt_small[0][None, :])
    log_decay = -jnp.exp(dt_small[1])[None, :] * dt_val
    return (xs, bcs[:, :N], bcs[:, N:], dt_val, log_decay)


def finish(y_local, xs, c_mat, cum_total, state_in, dt_small, gate_z):
    carried = jnp.einsum("tn,hpn->thp", c_mat, state_in, precision=highest)
    y_all = y_local + jnp.exp(cum_total)[:, :, None] * carried + dt_small[2][None, :, None] * xs
    return y_all.reshape(gate_z.shape) * jax.nn.silu(gate_z)


def full_local(proj_x, proj_bc, halo_rows, gate_z, dt_raw, x_conv, bc_conv, dt_small, state_in):
    xs, b_mat, c_mat, dt_val, log_decay = prepare(
        proj_x, proj_bc, halo_rows, x_conv, bc_conv, dt_small, dt_raw
    )
    y_local, s_local = ssd_run(xs, b_mat, c_mat, dt_val, log_decay, jnp.zeros_like(state_in))
    cum_total = jnp.cumsum(log_decay, axis=0)
    gated = finish(y_local, xs, c_mat, cum_total, state_in, dt_small, gate_z)
    state_out = jnp.exp(cum_total[-1])[:, None, None] * state_in + s_local
    return (gated, state_out)


def adamw(weight, moments, grad):
    moment_one = beta_one * moments[0] + (1.0 - beta_one) * grad
    root_two = jnp.sqrt(beta_two * moments[1] * moments[1] + (1.0 - beta_two) * grad * grad)
    first_hat = moment_one / (1.0 - beta_one**adam_step)
    root_hat = root_two / (1.0 - beta_two**adam_step) ** 0.5
    updated = weight - learn_rate * (first_hat / (root_hat + adam_eps) + decay_weight * weight)
    return (updated, jnp.stack([moment_one, root_two]))


def sum_small(parts):
    flat = jnp.concatenate([part.reshape(-1) for part in parts])
    count = flat.shape[0]
    rows = -(-count // 1024) * 8
    flat = jnp.pad(flat, (0, rows * 128 - count)).reshape(rows, 128)
    flat = sum_axis(sum_axis(flat, "seq"), "dp").reshape(-1)
    totals, at = [], 0
    for part in parts:
        totals.append(flat[at : at + part.size].reshape(part.shape))
        at += part.size
    return totals


def shards(
    hidden,
    cotangent,
    norm_gain,
    w_zx,
    w_bc,
    dt_table,
    x_conv,
    bc_conv,
    w_out,
    mom_norm,
    mom_zx,
    mom_bc,
    mom_table,
    mom_xconv,
    mom_bcconv,
    mom_out,
):
    owned = w_zx.shape[0]
    own_first = jnp.concatenate([w_zx[:, 1], w_bc], axis=1).astype(jnp.bfloat16)
    first_one = gather_axis(own_first, "dp")
    z_one = gather_axis(after(w_zx[:, 0].astype(jnp.bfloat16), first_one), "dp")
    first_full = spread_rows(first_one)
    out_one = gather_axis(after(w_out.T.astype(jnp.bfloat16), z_one), "dp")
    z_full = spread_rows(after(z_one, first_full))
    out_turned = spread_rows(after(out_one, z_full))
    half_inner = x_conv.shape[1]
    local_heads = dt_table.shape[1]
    head_dim = half_inner // local_heads
    num_seqs = hidden.shape[0]
    length = hidden.shape[1]
    rows = num_seqs * length
    resid = hidden.astype(jnp.float32).reshape(rows, D)
    inv_rms = lax.rsqrt(jnp.mean(resid * resid, axis=-1, keepdims=True) + norm_eps)
    normed = (resid * inv_rms * norm_gain[None, :]).astype(jnp.bfloat16)
    dt_mat = dt_table[:D].astype(jnp.bfloat16)
    dt_small = dt_table[D:]
    proj_first = jnp.dot(
        normed, jnp.concatenate([first_full, dt_mat], axis=1), preferred_element_type=jnp.float32
    )
    proj_x = proj_first[:, :half_inner].reshape(num_seqs, length, half_inner)
    proj_bc = proj_first[:, half_inner : half_inner + 2 * N].reshape(num_seqs, length, 2 * N)
    dt_raw = proj_first[:, half_inner + 2 * N :].reshape(num_seqs, length, local_heads)
    gate_z = jnp.dot(normed, z_full, preferred_element_type=jnp.float32)
    gate_z = gate_z.reshape(num_seqs, length, half_inner)
    rim_rows = jnp.concatenate(
        [proj_x[:, length - (CONV - 1) :], proj_bc[:, length - (CONV - 1) :]], axis=2
    )
    halo_rows = from_behind(rim_rows, "seq", 1)
    many_prepare = jax.vmap(prepare, in_axes=(0, 0, 0, None, None, None, 0))
    xs, b_mat, c_mat, dt_val, log_decay = many_prepare(
        proj_x, proj_bc, halo_rows, x_conv, bc_conv, dt_small, dt_raw
    )
    zero_state = jnp.zeros((local_heads, head_dim, N), jnp.float32)
    many_ssd = jax.vmap(ssd_run, in_axes=(0, 0, 0, 0, 0, None))
    y_local, s_local = many_ssd(xs, b_mat, c_mat, dt_val, log_decay, zero_state)
    cum_total = jnp.cumsum(log_decay, axis=1)
    decay_total = jnp.exp(cum_total[:, -1])
    decays = gather_axis(decay_total, "seq")
    state_in = entering(decays, s_local, "seq", False)
    many_finish = jax.vmap(finish, in_axes=(0, 0, 0, 0, 0, None, 0))
    gated = many_finish(y_local, xs, c_mat, cum_total, state_in, dt_small, gate_z).reshape(
        rows, half_inner
    )
    squares = with_partner(jnp.sum(gated * gated, axis=-1))
    inv_g = lax.rsqrt(squares / E + norm_eps)[:, None]
    gain_g = 1.0 + x_conv[CONV + 1][None, :]
    mixed = (gated * inv_g * gain_g).astype(jnp.bfloat16)
    partial_out = jnp.dot(mixed, out_turned.T, preferred_element_type=jnp.float32)
    branch = with_partner(partial_out)
    output = (resid + branch).astype(jnp.bfloat16).reshape(num_seqs, length, D)
    cot_tok = cotangent.reshape(rows, D)
    d_mixed = jnp.dot(cot_tok, out_turned, preferred_element_type=jnp.float32)
    grad_turned = jnp.dot(cot_tok.T, mixed, preferred_element_type=jnp.float32)
    own_g_out = scatter_rows(grad_turned).T
    scaled = d_mixed * gain_g
    gain_grad = jnp.sum(d_mixed * gated * inv_g, axis=0)
    cross = with_partner(jnp.sum(scaled * gated, axis=-1))
    d_gated = inv_g * scaled - gated * inv_g**3 / E * cross[:, None]
    d_gated_seq = d_gated.reshape(num_seqs, length, half_inner)
    d_core = (d_gated_seq * jax.nn.silu(gate_z)).reshape(num_seqs, length, local_heads, head_dim)
    g_state = jnp.einsum("sth,sthp,stn->shpn", jnp.exp(cum_total), d_core, c_mat, precision=highest)
    d_state_out = entering(decays, g_state, "seq", True)
    many_local = jax.vmap(full_local, in_axes=(0, 0, 0, 0, 0, None, None, None, 0))
    _, pull = jax.vjp(
        many_local, proj_x, proj_bc, halo_rows, gate_z, dt_raw, x_conv, bc_conv, dt_small, state_in
    )
    d_px, d_pbc, d_halo, d_gz, d_dr, g_xconv, g_bcconv, g_small, _ = pull(
        (d_gated_seq, d_state_out)
    )
    returned = from_behind(d_halo, "seq", -1)
    pad_rows = ((0, 0), (length - (CONV - 1), 0), (0, 0))
    d_px = (d_px + jnp.pad(returned[:, :, :half_inner], pad_rows)).reshape(rows, half_inner)
    d_pbc = (d_pbc + jnp.pad(returned[:, :, half_inner:], pad_rows)).reshape(rows, 2 * N)
    d_gz = d_gz.reshape(rows, half_inner)
    d_gz = d_gz.astype(jnp.bfloat16)
    d_px = d_px.astype(jnp.bfloat16)
    d_dt = d_dr.reshape(rows, local_heads).astype(jnp.bfloat16)
    own_g_z = scatter_rows(jnp.dot(normed.T, d_gz, preferred_element_type=jnp.float32))
    x_and_dt = jnp.concatenate([first_full[:, :half_inner], dt_mat], axis=1)
    d_part = jnp.dot(d_gz, z_full.T, preferred_element_type=jnp.float32) + jnp.dot(
        jnp.concatenate([d_px, d_dt], axis=1), x_and_dt.T, preferred_element_type=jnp.float32
    )
    d_heads, d_pbc_all, g_bcconv_all = (
        with_partner(d_part),
        with_partner(d_pbc),
        with_partner(g_bcconv),
    )
    d_bc = d_pbc_all.astype(jnp.bfloat16)
    d_normed = d_heads + jnp.dot(
        d_bc, first_full[:, half_inner:].T, preferred_element_type=jnp.float32)
    grad_proj = jnp.dot(
        normed.T, jnp.concatenate([d_px, d_bc], axis=1), preferred_element_type=jnp.float32
    )
    grad_dt = jnp.dot(d_dt.T, normed, preferred_element_type=jnp.float32)
    grad_norm = jnp.sum(d_normed * resid * inv_rms, axis=0)
    scaled_n = d_normed * norm_gain[None, :]
    d_hidden = (
        cot_tok.astype(jnp.float32)
        + inv_rms * scaled_n
        - resid * inv_rms**3 / D * jnp.sum(scaled_n * resid, axis=-1, keepdims=True)
    )
    grad_xconv = jnp.concatenate(
        [g_xconv[: CONV + 1], g_xconv[CONV + 1 :] + gain_grad[None, :]], axis=0
    )
    own_first = scatter_rows(grad_proj)
    own_g_zx = jnp.stack([own_g_z, own_first[:, :half_inner]], axis=1)
    own_g_bc = own_first[:, half_inner:]
    small = (grad_dt, g_small, grad_xconv, g_bcconv_all, grad_norm)
    total_dt, total_small, total_xconv, total_bcconv, total_norm = sum_small(small)
    total_table = jnp.concatenate([total_dt.T, total_small], axis=0)
    new_norm, new_mom_norm = adamw(norm_gain, mom_norm, total_norm)
    new_zx, new_mom_zx = adamw(w_zx, mom_zx, own_g_zx)
    new_bc, new_mom_bc = adamw(w_bc, mom_bc, own_g_bc)
    new_table, new_mom_table = adamw(dt_table, mom_table, total_table)
    new_xconv, new_mom_xconv = adamw(x_conv, mom_xconv, total_xconv)
    new_bcconv, new_mom_bcconv = adamw(bc_conv, mom_bcconv, total_bcconv)
    new_out, new_mom_out = adamw(w_out, mom_out, own_g_out)
    return (
        output,
        d_hidden.reshape(num_seqs, length, D),
        total_norm,
        own_g_zx,
        own_g_bc,
        total_table,
        total_xconv,
        total_bcconv,
        own_g_out,
        new_norm,
        new_zx,
        new_bc,
        new_table,
        new_xconv,
        new_bcconv,
        new_out,
        new_mom_norm,
        new_mom_zx,
        new_mom_bc,
        new_mom_table,
        new_mom_xconv,
        new_mom_bcconv,
        new_mom_out,
    )


def solution(mesh):
    placed = (
        P("dp", "seq", None),
        P("dp", "seq", None),
        P(),
        P(("dp", "seq"), None, "head"),
        P(("dp", "seq"), None),
        P(None, "head"),
        P(None, "head"),
        P(),
        P("head", ("dp", "seq")),
        P(),
        P(None, ("dp", "seq"), None, "head"),
        P(None, ("dp", "seq"), None),
        P(None, None, "head"),
        P(None, None, "head"),
        P(),
        P(None, "head", ("dp", "seq")),
    )
    return jax.shard_map(
        shards,
        mesh=mesh,
        in_specs=placed,
        out_specs=(
            P("dp", "seq", None),
            P("dp", "seq", None),
            P(),
            P(("dp", "seq"), None, "head"),
            P(("dp", "seq"), None),
            P(None, "head"),
            P(None, "head"),
            P(),
            P("head", ("dp", "seq")),
            P(),
            P(("dp", "seq"), None, "head"),
            P(("dp", "seq"), None),
            P(None, "head"),
            P(None, "head"),
            P(),
            P("head", ("dp", "seq")),
            P(),
            P(None, ("dp", "seq"), None, "head"),
            P(None, ("dp", "seq"), None),
            P(None, None, "head"),
            P(None, None, "head"),
            P(),
            P(None, "head", ("dp", "seq")),
        ),
        check_vma=False,
    )
```

```python
import jax
import jax.numpy as jnp
from jax import lax
from jax.sharding import PartitionSpec as P

D = 768
E = 1536
N = 128
CONV = 4
BLOCK = 256


norm_eps = 1e-05
learn_rate = 0.01
beta_one = 0.9
beta_two = 0.95
adam_eps = 1e-08
decay_weight = 0.1
adam_step = 10.0
far_below = -1e30
highest = lax.Precision.HIGH


def from_behind(block, axis, distance):
    devices = range(lax.axis_size(axis))
    route = [(i - distance, i) for i in devices if i - distance in devices]
    return lax.ppermute(block, axis, route)


def turn(block, axis, distance):
    count = lax.axis_size(axis)
    return lax.ppermute(block, axis, [(i, (i + distance) % count) for i in range(count)])


def gather_axis(block, axis):
    count = lax.axis_size(axis)
    place = lax.axis_index(axis)
    whole = jnp.zeros((count,) + block.shape, block.dtype)
    for distance in range(count):
        part = turn(block, axis, distance) if distance else block
        source = lax.rem(place - distance + count, count)
        whole = lax.dynamic_update_index_in_dim(whole, part, source, 0)
    return whole


def scatter_axis(blocks, axis):
    count = lax.axis_size(axis)
    place = lax.axis_index(axis)
    total = None
    for distance in range(count):
        target = lax.rem(place + distance, count)
        part = lax.dynamic_index_in_dim(blocks, target, 0, False)
        part = turn(part.astype(jnp.bfloat16), axis, distance) if distance else part
        part = part.astype(jnp.float32)
        total = part if total is None else total + part
    return total


def sum_axis(block, axis):
    total = block
    for distance in range(1, lax.axis_size(axis)):
        total = total + turn(block, axis, distance)
    return total


def after(block, other):
    return lax.optimization_barrier((block, other))[0]


def spread_rows(stage_one):
    by_seq = gather_axis(stage_one, "seq")
    return jnp.swapaxes(by_seq, 0, 1).reshape(-1, stage_one.shape[-1])


def scatter_rows(grads):
    dp, seq = lax.axis_size("dp"), lax.axis_size("seq")
    blocks = grads.reshape(dp, seq, grads.shape[0] // (dp * seq), grads.shape[1])
    by_seq = scatter_axis(jnp.swapaxes(blocks, 0, 1), "seq")
    return scatter_axis(by_seq, "dp")


def with_partner(block):
    return block + turn(block, "head", 1)


def entering(decays, state, axis, reverse):
    sign = -1 if reverse else 1
    distances = range(1, lax.axis_size(axis))
    sent = state.astype(jnp.bfloat16)
    states = [from_behind(sent, axis, sign * d).astype(jnp.float32) for d in distances]
    place = lax.axis_index(axis)
    total = jnp.zeros_like(state)
    for d in reversed(distances):
        source = jnp.clip(place - sign * d, 0, lax.axis_size(axis) - 1)
        passed = lax.dynamic_index_in_dim(decays, source, 0, False)
        total = passed[..., None, None] * total + states[d - 1]
    return total


def running_sum(values):
    length = values.shape[-2]
    lower = jnp.tril(jnp.ones((length, length), jnp.float32))
    return jnp.einsum("ts,...sh->...th", lower, values, precision=lax.Precision.HIGHEST)


def conv_silu(signal, halo_rows, taps, shift_bias):
    padded = jnp.concatenate([halo_rows, signal], axis=0)
    length = signal.shape[0]
    total = jnp.broadcast_to(shift_bias[None, :], signal.shape)
    for offset in range(taps.shape[0]):
        total = total + taps[offset][None, :] * padded[offset : offset + length]
    return jax.nn.silu(total)


def block_step(state, block_data):
    x_block, b_block, c_block, dt_block, log_block = block_data
    cum_log = running_sum(log_block)
    length = x_block.shape[0]
    row_ids = lax.broadcasted_iota(jnp.int32, (length, length), 0)
    col_ids = lax.broadcasted_iota(jnp.int32, (length, length), 1)
    causal = (row_ids >= col_ids)[:, :, None]
    spread = cum_log[:, None, :] - cum_log[None, :, :]
    decay_mat = jnp.exp(jnp.where(causal, spread, far_below))
    inner = jnp.dot(c_block, b_block.T, precision=highest)
    mixing = inner[:, :, None] * decay_mat * dt_block[None, :, :]
    y_block = jnp.einsum("tsh,shp->thp", mixing, x_block, precision=highest)
    carried = jnp.einsum("tn,hpn->thp", c_block, state, precision=highest)
    y_block = y_block + jnp.exp(cum_log)[:, :, None] * carried
    tail_weight = jnp.exp(cum_log[-1][None, :] - cum_log) * dt_block
    fresh = jnp.einsum("sh,shp,sn->hpn", tail_weight, x_block, b_block, precision=highest)
    new_state = jnp.exp(cum_log[-1])[:, None, None] * state + fresh
    return (new_state, y_block)


def ssd_run(inputs_x, b_mat, c_mat, dt_val, log_decay, start_state):
    tokens, num_heads, head_dim = inputs_x.shape
    blocks = tokens // BLOCK
    pieces = (
        inputs_x.reshape(blocks, BLOCK, num_heads, head_dim),
        b_mat.reshape(blocks, BLOCK, b_mat.shape[1]),
        c_mat.reshape(blocks, BLOCK, c_mat.shape[1]),
        dt_val.reshape(blocks, BLOCK, num_heads),
        log_decay.reshape(blocks, BLOCK, num_heads),
    )
    final_state, outputs = lax.scan(block_step, start_state, pieces)
    return (outputs.reshape(tokens, num_heads, head_dim), final_state)


def prepare(proj_x, proj_bc, halo_rows, x_conv, bc_conv, dt_small, dt_raw):
    tokens, inner_width = proj_x.shape
    num_heads = dt_small.shape[1]
    xs = conv_silu(proj_x, halo_rows[:, :inner_width], x_conv[:CONV], x_conv[CONV])
    xs = xs.reshape(tokens, num_heads, inner_width // num_heads)
    bcs = conv_silu(proj_bc, halo_rows[:, inner_width:], bc_conv[:CONV], bc_conv[CONV])
    dt_val = jax.nn.softplus(dt_raw + dt_small[0][None, :])
    log_decay = -jnp.exp(dt_small[1])[None, :] * dt_val
    return (xs, bcs[:, :N], bcs[:, N:], dt_val, log_decay)


def finish(y_local, xs, c_mat, cum_total, state_in, dt_small, gate_z):
    carried = jnp.einsum("tn,hpn->thp", c_mat, state_in, precision=highest)
    y_all = y_local + jnp.exp(cum_total)[:, :, None] * carried + dt_small[2][None, :, None] * xs
    return y_all.reshape(gate_z.shape) * jax.nn.silu(gate_z)


def full_local(proj_x, proj_bc, halo_rows, gate_z, dt_raw, x_conv, bc_conv, dt_small, state_in):
    xs, b_mat, c_mat, dt_val, log_decay = prepare(
        proj_x, proj_bc, halo_rows, x_conv, bc_conv, dt_small, dt_raw
    )
    y_local, s_local = ssd_run(xs, b_mat, c_mat, dt_val, log_decay, jnp.zeros_like(state_in))
    cum_total = running_sum(log_decay)
    gated = finish(y_local, xs, c_mat, cum_total, state_in, dt_small, gate_z)
    state_out = jnp.exp(cum_total[-1])[:, None, None] * state_in + s_local
    return (gated, state_out)


def adamw(weight, moments, grad):
    moment_one = beta_one * moments[0] + (1.0 - beta_one) * grad
    root_two = jnp.sqrt(beta_two * moments[1] * moments[1] + (1.0 - beta_two) * grad * grad)
    first_hat = moment_one / (1.0 - beta_one**adam_step)
    root_hat = root_two / (1.0 - beta_two**adam_step) ** 0.5
    updated = weight - learn_rate * (first_hat / (root_hat + adam_eps) + decay_weight * weight)
    return (updated, jnp.stack([moment_one, root_two]))


def sum_small(parts):
    flat = jnp.concatenate([part.reshape(-1) for part in parts])
    count = flat.shape[0]
    rows = -(-count // 1024) * 8
    flat = jnp.pad(flat, (0, rows * 128 - count)).reshape(rows, 128)
    flat = sum_axis(sum_axis(flat, "seq"), "dp").reshape(-1)
    totals, at = [], 0
    for part in parts:
        totals.append(flat[at : at + part.size].reshape(part.shape))
        at += part.size
    return totals


def shards(
    hidden,
    cotangent,
    norm_gain,
    w_zx,
    w_bc,
    dt_table,
    x_conv,
    bc_conv,
    w_out,
    mom_norm,
    mom_zx,
    mom_bc,
    mom_table,
    mom_xconv,
    mom_bcconv,
    mom_out,
):
    owned = w_zx.shape[0]
    own_first = jnp.concatenate([w_zx[:, 1], w_bc], axis=1).astype(jnp.bfloat16)
    first_one = gather_axis(own_first, "dp")
    own_later = jnp.concatenate([w_zx[:, 0], w_out.T], axis=1).astype(jnp.bfloat16)
    later_one = gather_axis(after(own_later, first_one), "dp")
    first_full = spread_rows(first_one)
    later_full = spread_rows(after(later_one, first_full))
    z_full = later_full[:, : x_conv.shape[1]]
    out_turned = later_full[:, x_conv.shape[1] :]
    half_inner = x_conv.shape[1]
    local_heads = dt_table.shape[1]
    head_dim = half_inner // local_heads
    num_seqs = hidden.shape[0]
    length = hidden.shape[1]
    rows = num_seqs * length
    resid = hidden.astype(jnp.float32).reshape(rows, D)
    inv_rms = lax.rsqrt(jnp.mean(resid * resid, axis=-1, keepdims=True) + norm_eps)
    normed = (resid * inv_rms * norm_gain[None, :]).astype(jnp.bfloat16)
    dt_mat = dt_table[:D].astype(jnp.bfloat16)
    dt_small = dt_table[D:]
    proj_first = jnp.dot(
        normed, jnp.concatenate([first_full, dt_mat], axis=1), preferred_element_type=jnp.float32
    )
    proj_x = proj_first[:, :half_inner].reshape(num_seqs, length, half_inner)
    proj_bc = proj_first[:, half_inner : half_inner + 2 * N].reshape(num_seqs, length, 2 * N)
    dt_raw = proj_first[:, half_inner + 2 * N :].reshape(num_seqs, length, local_heads)
    gate_z = jnp.dot(normed, z_full, preferred_element_type=jnp.float32)
    gate_z = gate_z.reshape(num_seqs, length, half_inner)
    rim_rows = jnp.concatenate(
        [proj_x[:, length - (CONV - 1) :], proj_bc[:, length - (CONV - 1) :]], axis=2
    )
    halo_rows = from_behind(rim_rows, "seq", 1)
    many_prepare = jax.vmap(prepare, in_axes=(0, 0, 0, None, None, None, 0))
    xs, b_mat, c_mat, dt_val, log_decay = many_prepare(
        proj_x, proj_bc, halo_rows, x_conv, bc_conv, dt_small, dt_raw
    )
    zero_state = jnp.zeros((local_heads, head_dim, N), jnp.float32)
    many_ssd = jax.vmap(ssd_run, in_axes=(0, 0, 0, 0, 0, None))
    y_local, s_local = many_ssd(xs, b_mat, c_mat, dt_val, log_decay, zero_state)
    cum_total = running_sum(log_decay)
    decay_total = jnp.exp(cum_total[:, -1])
    decays = gather_axis(decay_total, "seq")
    state_in = entering(decays, s_local, "seq", False)
    many_finish = jax.vmap(finish, in_axes=(0, 0, 0, 0, 0, None, 0))
    gated = many_finish(y_local, xs, c_mat, cum_total, state_in, dt_small, gate_z).reshape(
        rows, half_inner
    )
    squares = with_partner(jnp.sum(gated * gated, axis=-1))
    inv_g = lax.rsqrt(squares / E + norm_eps)[:, None]
    gain_g = 1.0 + x_conv[CONV + 1][None, :]
    mixed = (gated * inv_g * gain_g).astype(jnp.bfloat16)
    partial_out = jnp.dot(mixed, out_turned.T, preferred_element_type=jnp.float32)
    branch = with_partner(partial_out)
    output = (resid + branch).astype(jnp.bfloat16).reshape(num_seqs, length, D)
    cot_tok = cotangent.reshape(rows, D)
    d_mixed = jnp.dot(cot_tok, out_turned, preferred_element_type=jnp.float32)
    grad_turned = jnp.dot(cot_tok.T, mixed, preferred_element_type=jnp.float32)
    scaled = d_mixed * gain_g
    gain_grad = jnp.sum(d_mixed * gated * inv_g, axis=0)
    cross = with_partner(jnp.sum(scaled * gated, axis=-1))
    d_gated = inv_g * scaled - gated * inv_g**3 / E * cross[:, None]
    d_gated_seq = d_gated.reshape(num_seqs, length, half_inner)
    d_core = (d_gated_seq * jax.nn.silu(gate_z)).reshape(num_seqs, length, local_heads, head_dim)
    g_state = jnp.einsum("sth,sthp,stn->shpn", jnp.exp(cum_total), d_core, c_mat, precision=highest)
    d_state_out = entering(decays, g_state, "seq", True)
    many_local = jax.vmap(full_local, in_axes=(0, 0, 0, 0, 0, None, None, None, 0))
    _, pull = jax.vjp(
        many_local, proj_x, proj_bc, halo_rows, gate_z, dt_raw, x_conv, bc_conv, dt_small, state_in
    )
    d_px, d_pbc, d_halo, d_gz, d_dr, g_xconv, g_bcconv, g_small, _ = pull(
        (d_gated_seq, d_state_out)
    )
    returned = from_behind(d_halo, "seq", -1)
    pad_rows = ((0, 0), (length - (CONV - 1), 0), (0, 0))
    d_px = (d_px + jnp.pad(returned[:, :, :half_inner], pad_rows)).reshape(rows, half_inner)
    d_pbc = (d_pbc + jnp.pad(returned[:, :, half_inner:], pad_rows)).reshape(rows, 2 * N)
    d_gz = d_gz.reshape(rows, half_inner)
    d_gz = d_gz.astype(jnp.bfloat16)
    d_px = d_px.astype(jnp.bfloat16)
    d_dt = d_dr.reshape(rows, local_heads).astype(jnp.bfloat16)
    grad_z = jnp.dot(normed.T, d_gz, preferred_element_type=jnp.float32)
    own_later_g = scatter_rows(jnp.concatenate([grad_z, grad_turned], axis=1))
    own_g_z = own_later_g[:, :half_inner]
    own_g_out = own_later_g[:, half_inner:].T
    x_and_dt = jnp.concatenate([first_full[:, :half_inner], dt_mat], axis=1)
    d_part = jnp.dot(d_gz, z_full.T, preferred_element_type=jnp.float32) + jnp.dot(
        jnp.concatenate([d_px, d_dt], axis=1), x_and_dt.T, preferred_element_type=jnp.float32
    )
    d_heads = with_partner(d_part)
    bc_and_conv = with_partner(jnp.concatenate([d_pbc, g_bcconv], axis=0))
    d_pbc_all, g_bcconv_all = bc_and_conv[:rows], bc_and_conv[rows:]
    d_bc = d_pbc_all.astype(jnp.bfloat16)
    d_normed = d_heads + jnp.dot(
        d_bc, first_full[:, half_inner:].T, preferred_element_type=jnp.float32)
    grad_proj = jnp.dot(
        normed.T, jnp.concatenate([d_px, d_bc], axis=1), preferred_element_type=jnp.float32
    )
    grad_dt = jnp.dot(d_dt.T, normed, preferred_element_type=jnp.float32)
    grad_norm = jnp.sum(d_normed * resid * inv_rms, axis=0)
    scaled_n = d_normed * norm_gain[None, :]
    d_hidden = (
        cot_tok.astype(jnp.float32)
        + inv_rms * scaled_n
        - resid * inv_rms**3 / D * jnp.sum(scaled_n * resid, axis=-1, keepdims=True)
    )
    grad_xconv = jnp.concatenate(
        [g_xconv[: CONV + 1], g_xconv[CONV + 1 :] + gain_grad[None, :]], axis=0
    )
    own_first = scatter_rows(grad_proj)
    own_g_zx = jnp.stack([own_g_z, own_first[:, :half_inner]], axis=1)
    own_g_bc = own_first[:, half_inner:]
    small = (grad_dt, g_small, grad_xconv, g_bcconv_all, grad_norm)
    total_dt, total_small, total_xconv, total_bcconv, total_norm = sum_small(small)
    total_table = jnp.concatenate([total_dt.T, total_small], axis=0)
    new_norm, new_mom_norm = adamw(norm_gain, mom_norm, total_norm)
    new_zx, new_mom_zx = adamw(w_zx, mom_zx, own_g_zx)
    new_bc, new_mom_bc = adamw(w_bc, mom_bc, own_g_bc)
    new_table, new_mom_table = adamw(dt_table, mom_table, total_table)
    new_xconv, new_mom_xconv = adamw(x_conv, mom_xconv, total_xconv)
    new_bcconv, new_mom_bcconv = adamw(bc_conv, mom_bcconv, total_bcconv)
    new_out, new_mom_out = adamw(w_out, mom_out, own_g_out)
    return (
        output,
        d_hidden.reshape(num_seqs, length, D),
        total_norm,
        own_g_zx,
        own_g_bc,
        total_table,
        total_xconv,
        total_bcconv,
        own_g_out,
        new_norm,
        new_zx,
        new_bc,
        new_table,
        new_xconv,
        new_bcconv,
        new_out,
        new_mom_norm,
        new_mom_zx,
        new_mom_bc,
        new_mom_table,
        new_mom_xconv,
        new_mom_bcconv,
        new_mom_out,
    )


def solution(mesh):
    placed = (
        P("dp", "seq", None),
        P("dp", "seq", None),
        P(),
        P(("dp", "seq"), None, "head"),
        P(("dp", "seq"), None),
        P(None, "head"),
        P(None, "head"),
        P(),
        P("head", ("dp", "seq")),
        P(),
        P(None, ("dp", "seq"), None, "head"),
        P(None, ("dp", "seq"), None),
        P(None, None, "head"),
        P(None, None, "head"),
        P(),
        P(None, "head", ("dp", "seq")),
    )
    return jax.shard_map(
        shards,
        mesh=mesh,
        in_specs=placed,
        out_specs=(
            P("dp", "seq", None),
            P("dp", "seq", None),
            P(),
            P(("dp", "seq"), None, "head"),
            P(("dp", "seq"), None),
            P(None, "head"),
            P(None, "head"),
            P(),
            P("head", ("dp", "seq")),
            P(),
            P(("dp", "seq"), None, "head"),
            P(("dp", "seq"), None),
            P(None, "head"),
            P(None, "head"),
            P(),
            P("head", ("dp", "seq")),
            P(),
            P(None, ("dp", "seq"), None, "head"),
            P(None, ("dp", "seq"), None),
            P(None, None, "head"),
            P(None, None, "head"),
            P(),
            P(None, "head", ("dp", "seq")),
        ),
        check_vma=False,
    )
```
